32 devices in a mesh: rows: 8 (over z, x), chan: 4 (over y, core).
Axes of the slice: x: 2, y: 2, z: 4, core: 2. Of those that a mesh axis runs over, the one named last changes fastest.
Arguments:
- pair_act: bfloat16 [128, 768, 768], P('chan', 'rows'), may hold values from -16 to 16
- pair_cot: bfloat16 [128, 768, 768], P('chan', 'rows'), may hold values from -1.5 to 1.5
- contact: int32 [6, 6], replicated, may hold values from 0 to 1, as said below
- ln_gain: float32 [128], replicated, may hold values from 0.5 to 2
- ln_bias: float32 [128], replicated, may hold values from -2 to 2
- left_gate: bfloat16 [128, 128], P(None, 'chan'), may hold values from -0.5 to 0.5
- left_value: bfloat16 [128, 128], P(None, 'chan'), may hold values from -0.5 to 0.5
- right_gate: bfloat16 [128, 128], P(None, 'chan'), may hold values from -0.5 to 0.5
- right_value: bfloat16 [128, 128], P(None, 'chan'), may hold values from -0.5 to 0.5
Outputs:
- pair_grad: bfloat16 [128, 768, 768], P('chan', 'rows')
- gain_grad: float32 [128], P('chan')
- bias_grad: float32 [128], P('chan')
- left_gate_grad: float32 [128, 128], P(None, 'chan')
- left_value_grad: float32 [128, 128], P(None, 'chan')
- right_gate_grad: float32 [128, 128], P(None, 'chan')
- right_value_grad: float32 [128, 128], P(None, 'chan')
The draws below stay inside these ranges and needn't reach their ends.
Inputs may be any that keep to these rules, and one draw needn't show every extreme that they name: `contact`: each block row has 1 to 2 active blocks, its diagonal block always among them; block row 0 has exactly 2.
All inputs are finite; a program needn't handle non-finite values.
Results may differ from the reference program's by a relative error of at most 0.0068.
Values may be sent and summed in bfloat16 or wider, within the bound.
A program may use at most 256 MiB of HBM per device.

```python
import math
import jax
import jax.numpy as jnp
from jax import lax

C = 128
HID = 128
BT = 128
CAP = 2
NTOK = 768
NB = 6


def draw_contact(key, part):
    first_key, second_key = jax.random.split(jax.random.fold_in(key, 7))
    positions = jnp.arange(NB, dtype=jnp.int32)
    counts = jax.random.randint(first_key, (NB,), 1, CAP + 1, dtype=jnp.int32)
    counts = jnp.where(positions == 0, CAP, counts)
    scores = jax.random.randint(second_key, (NB, NB), 0, 1 << 20, dtype=jnp.int32) * NB + positions[None, :]
    scores = jnp.where(positions[:, None] == positions[None, :], (1 << 20) * NB + NB, scores)
    order = jnp.argsort(-scores, axis=1)
    ranks = jnp.argsort(order, axis=1)
    return (ranks < counts[:, None]).astype(jnp.int32)


def draw_pair_act(key, part):
    first_key, second_key = jax.random.split(jax.random.fold_in(key, 11), 2)
    chan_scale = jnp.exp(jax.random.uniform(first_key, (C, 1, 1), jnp.float32, math.log(0.3), math.log(3.0)))
    base = jax.random.normal(second_key, (C, NTOK, NTOK), jnp.float32)
    values = base * chan_scale
    return jnp.clip(values, -16.0, 16.0).astype(jnp.bfloat16)


def block_scale(rng, extent, cuts, least, largest):
    level = 1.0
    for dim, shards_of in cuts:
        heights = jax.random.uniform(jax.random.fold_in(jax.random.fold_in(rng, 6), dim), (shards_of,), jnp.float32, least / len(cuts), largest / len(cuts))
        level = level * jnp.repeat(jnp.exp(heights), extent[dim] // shards_of).reshape((-1,) + (1,) * (len(extent) - 1 - dim))
    return level


def gaussian(own_key, shape, scale, limit, shards=(), kind=jnp.bfloat16):
    result = scale * jax.random.normal(own_key, shape, jnp.float32)
    if shards:
        result = result * block_scale(own_key, shape, shards, -0.22, 0.18)
    return jnp.clip(result, -limit, limit).astype(kind)


def setup_inputs(seed: int = 0) -> dict:
    arg_keys = jax.random.split(jax.random.key(seed), 10)
    return {
        "pair_act": draw_pair_act(jax.random.fold_in(arg_keys[9], 71), 0),
        "pair_cot": gaussian(arg_keys[1], (HID, NTOK, NTOK), 0.25, 1.5, ((0, 4), (1, 8))),
        "contact": draw_contact(jax.random.fold_in(arg_keys[9], 71), 0),
        "ln_gain": jnp.clip(jnp.exp(jax.random.uniform(arg_keys[3], (C,), jnp.float32, math.log(0.5), math.log(2.0))), 0.5, 2.0),
        "ln_bias": gaussian(arg_keys[4], (C,), 0.5, 2.0, (), jnp.float32),
        "left_gate": gaussian(arg_keys[5], (C, HID), C ** -0.5, 0.5, ((1, 4),)),
        "left_value": gaussian(arg_keys[6], (C, HID), C ** -0.5, 0.5, ((1, 4),)),
        "right_gate": gaussian(arg_keys[7], (C, HID), C ** -0.5, 0.5, ((1, 4),)),
        "right_value": gaussian(arg_keys[8], (C, HID), C ** -0.5, 0.5, ((1, 4),)),
    }


EPS = 1e-05

def reference(pair_act, pair_cot, contact, ln_gain, ln_bias, left_gate, left_value, right_gate, right_value):
    block_mask = contact.astype(jnp.float32)
    pair_mask = jnp.repeat(jnp.repeat(block_mask, BT, axis=0), BT, axis=1)
    values = pair_act.astype(jnp.float32)
    mean = lax.optimization_barrier(jnp.mean(values, axis=0))
    inv_std = lax.rsqrt(lax.optimization_barrier(jnp.mean(values * values, axis=0)) - mean * mean + EPS)
    standard = (values - mean) * inv_std
    normed = (standard * ln_gain[:, None, None] + ln_bias[:, None, None]).astype(jnp.bfloat16)
    normed_wide = normed.astype(jnp.float32)

    def project(weight):
        return jnp.einsum('ch,ckn->hkn', weight.astype(jnp.float32), normed_wide)
    left_logit = project(left_gate)
    left_linear = project(left_value)
    right_logit = project(right_gate)
    right_linear = project(right_value)
    left_sigmoid = jax.nn.sigmoid(left_logit)
    right_sigmoid = jax.nn.sigmoid(right_logit)
    left = (pair_mask * left_sigmoid * left_linear).astype(jnp.bfloat16)
    right = (pair_mask * right_sigmoid * right_linear).astype(jnp.bfloat16)
    masked_cot = pair_cot.astype(jnp.float32) * pair_mask
    grad_left = jnp.einsum('hkj,hij->hki', right.astype(jnp.float32), masked_cot)
    grad_right = jnp.einsum('hki,hij->hkj', left.astype(jnp.float32), masked_cot)
    keep_left = grad_left * pair_mask
    keep_right = grad_right * pair_mask
    left_logit_grad = (keep_left * left_linear * left_sigmoid * (1.0 - left_sigmoid)).astype(jnp.bfloat16)
    left_linear_grad = (keep_left * left_sigmoid).astype(jnp.bfloat16)
    right_logit_grad = (keep_right * right_linear * right_sigmoid * (1.0 - right_sigmoid)).astype(jnp.bfloat16)
    right_linear_grad = (keep_right * right_sigmoid).astype(jnp.bfloat16)

    def back(weight, grad):
        return jnp.einsum('ch,hkn->ckn', weight.astype(jnp.float32), grad.astype(jnp.float32))
    normed_grad = back(left_gate, left_logit_grad) + back(left_value, left_linear_grad)
    normed_grad = normed_grad + back(right_gate, right_logit_grad) + back(right_value, right_linear_grad)
    scaled = normed_grad * ln_gain[:, None, None]
    first_mean = lax.optimization_barrier(jnp.mean(scaled, axis=0))
    second_mean = lax.optimization_barrier(jnp.mean(scaled * standard, axis=0))
    pair_grad = ((scaled - first_mean - standard * second_mean) * inv_std).astype(jnp.bfloat16)
    factor = 1.0 / NTOK
    gain_grad = lax.optimization_barrier(jnp.sum(normed_grad * standard, axis=(1, 2))) * factor
    bias_grad = lax.optimization_barrier(jnp.sum(normed_grad, axis=(1, 2))) * factor

    def weight_grad(grad):
        return jnp.einsum('ckn,hkn->ch', normed_wide, grad.astype(jnp.float32)) * factor
    return (pair_grad, gain_grad, bias_grad, weight_grad(left_logit_grad), weight_grad(left_linear_grad), weight_grad(right_logit_grad), weight_grad(right_linear_grad))
```

```python
import math

import jax
import jax.numpy as jnp
from jax import lax
from jax.sharding import PartitionSpec as P

EPS = 1e-05


def ring_order(count):
    return list(range(0, count, 2)) + list(range(1, count, 2))[::-1]


def flip(x, axis, bit):
    count = lax.axis_size(axis)
    return lax.ppermute(x, axis, [(d, d ^ bit) for d in range(count)])


def bits_down(count):
    bits = [1 << b for b in range(count.bit_length() - 1)]
    return bits[::-1]


def local(
    pair_act, pair_cot, contact, ln_gain, ln_bias, left_gate, left_value, right_gate, right_value
):
    part_chan, rows_here, width = pair_act.shape
    part_hid = pair_cot.shape[0]
    blocks = contact.shape[0]
    block_len = width // blocks
    chans = lax.axis_size("chan")
    ring = lax.axis_size("rows")
    all_chan = part_chan * chans
    mine = lax.axis_index("chan")
    row_first = lax.axis_index("rows") * rows_here
    piece = math.gcd(rows_here, block_len)
    pieces = rows_here // piece

    numbers = jnp.arange(blocks, dtype=jnp.int32)
    other = jnp.sum(contact * numbers[None, :], axis=1) - numbers
    paired = jnp.sum(contact, axis=1) > 1
    row_block = (row_first + jnp.arange(rows_here, dtype=jnp.int32)) // block_len
    at_own = row_block[:, None] == numbers[None, :]
    row_other = jnp.sum(jnp.where(at_own, other[None, :], 0), axis=1)
    row_paired = jnp.sum(jnp.where(at_own, paired[None, :].astype(jnp.int32), 0), axis=1) > 0
    at_other = (row_other[:, None] == numbers[None, :]) & row_paired[:, None]
    weight = jnp.concatenate(
        [
            jnp.ones((rows_here, block_len), jnp.float32),
            jnp.broadcast_to(
                row_paired.astype(jnp.float32)[:, None], (rows_here, block_len)
            ),
        ],
        axis=1,
    )

    def compact(x):
        def pick(at):
            out = jnp.zeros((x.shape[0], rows_here, block_len), x.dtype)
            for b in range(blocks):
                here = x[:, :, b * block_len : (b + 1) * block_len]
                out = jnp.where(at[:, b][None, :, None], here, out)
            return out

        return jnp.concatenate([pick(at_own), pick(at_other)], axis=2)

    cot = compact(pair_cot)
    order = ring_order(ring)
    place = [order.index(d) for d in range(ring)]
    order_table = jnp.array(order, jnp.int32)
    my_place = jnp.array(place, jnp.int32)[lax.axis_index("rows")]
    right_perm = [(order[i], order[(i + 1) % ring]) for i in range(ring)]
    left_perm = [(order[(i + 1) % ring], order[i]) for i in range(ring)]
    act = compact(pair_act)
    gathered = jnp.zeros((part_hid, width, 2 * block_len), cot.dtype)
    gathered = lax.dynamic_update_slice(gathered, cot, (0, row_first, 0))
    going_right, going_left = cot, cot
    for step in range(1, ring // 2 + 1):
        going_right = lax.ppermute(going_right, "rows", right_perm)
        source = order_table[(my_place - step + ring) % ring]
        gathered = lax.dynamic_update_slice(gathered, going_right, (0, source * rows_here, 0))
        if step < ring - ring // 2:
            going_left = lax.ppermute(going_left, "rows", left_perm)
            source = order_table[(my_place + step) % ring]
            gathered = lax.dynamic_update_slice(
                gathered, going_left, (0, source * rows_here, 0)
            )

    parts, offsets = [act], [0]
    for bit in bits_down(chans):
        parts = parts + [flip(x, "chan", bit) for x in parts]
        offsets = offsets + [o + bit for o in offsets]
    full_act = jnp.concatenate(parts, axis=0).astype(jnp.float32)
    partner = jnp.array(offsets, jnp.int32) ^ mine

    def by_partner(x):
        return x.reshape((chans, part_chan) + x.shape[1:])[partner].reshape(x.shape)

    slot_of = [offsets.index(o) for o in range(chans)]
    back_order = jnp.array(slot_of, jnp.int32)[jnp.arange(chans, dtype=jnp.int32) ^ mine]

    def by_channel(x):
        return x.reshape((chans, part_chan) + x.shape[1:])[back_order].reshape(x.shape)

    gain = by_partner(ln_gain)
    bias = by_partner(ln_bias)
    w_stacked = by_partner(
        jnp.concatenate([left_gate, left_value, right_gate, right_value], axis=1)
    )

    mean = jnp.mean(full_act, axis=0)
    inv_std = lax.rsqrt(jnp.mean(full_act * full_act, axis=0) - mean * mean + EPS)
    standard = (full_act - mean) * inv_std
    normed = (standard * gain[:, None, None] + bias[:, None, None]).astype(jnp.bfloat16)
    standard_near = standard.astype(jnp.bfloat16)
    projected = jnp.einsum("ch,ckn->hkn", w_stacked, normed, preferred_element_type=jnp.float32)
    left_logit, left_linear, right_logit, right_linear = jnp.split(projected, 4, axis=0)
    left_sigmoid = jax.nn.sigmoid(left_logit)
    right_sigmoid = jax.nn.sigmoid(right_logit)
    left = (weight * left_sigmoid * left_linear).astype(jnp.bfloat16)
    right = (weight * right_sigmoid * right_linear).astype(jnp.bfloat16)

    corners = []
    for p in range(pieces):
        own = (row_first + p * piece) // block_len
        second = other[own]
        mutual = paired[second] & (other[second] == own)
        top = lax.dynamic_slice(
            gathered, (0, own * block_len, 0), (part_hid, block_len, 2 * block_len)
        )
        low = lax.dynamic_slice(
            gathered, (0, second * block_len, 0), (part_hid, block_len, 2 * block_len)
        )
        low = jnp.concatenate(
            [
                jnp.where(mutual, low[:, :, block_len:], jnp.zeros((), low.dtype)),
                low[:, :, :block_len],
            ],
            axis=2,
        )
        corners.append(jnp.concatenate([top, low], axis=1))
    corner = jnp.stack(corners, axis=1)

    def cut(x):
        return x.reshape(part_hid, pieces, piece, 2 * block_len)

    grad_left = jnp.einsum(
        "hpkj,hpij->hpki", cut(right), corner, preferred_element_type=jnp.float32
    ).reshape(left.shape)
    grad_right = jnp.einsum(
        "hpki,hpij->hpkj", cut(left), corner, preferred_element_type=jnp.float32
    ).reshape(left.shape)
    keep_left = grad_left * weight
    keep_right = grad_right * weight
    grads = jnp.concatenate(
        [
            (keep_left * left_linear * left_sigmoid * (1.0 - left_sigmoid)).astype(jnp.bfloat16),
            (keep_left * left_sigmoid).astype(jnp.bfloat16),
            (keep_right * right_linear * right_sigmoid * (1.0 - right_sigmoid)).astype(
                jnp.bfloat16
            ),
            (keep_right * right_sigmoid).astype(jnp.bfloat16),
        ],
        axis=0,
    )

    def back(rows):
        return jnp.einsum("ch,hkn->ckn", rows, grads, preferred_element_type=jnp.float32)

    w_parts = {o: w_stacked[i * part_chan : (i + 1) * part_chan] for i, o in enumerate(offsets)}
    partial = {o: back(w_parts[o]) for o in offsets}
    first_sum = jnp.zeros(mean.shape, jnp.float32)
    second_sum = jnp.zeros(mean.shape, jnp.float32)
    for i, o in enumerate(offsets):
        span = slice(i * part_chan, (i + 1) * part_chan)
        scaled = partial[o] * gain[span][:, None, None]
        first_sum = first_sum + jnp.sum(scaled, axis=0)
        second_sum = second_sum + jnp.sum(scaled * standard[span], axis=0)
    sums = jnp.stack([first_sum, second_sum])
    for bit in bits_down(chans)[::-1]:
        received = {
            o - bit: flip(partial[o].astype(jnp.bfloat16), "chan", bit)
            for o in partial
            if o & bit
        }
        partial = {o: partial[o] + x.astype(jnp.float32) for o, x in received.items()}
        sums = sums + flip(sums, "chan", bit)
    normed_grad = partial[0]
    scaled = normed_grad * gain[:part_chan][:, None, None]
    pair_grad = (
        (scaled - sums[0] / all_chan - standard[:part_chan] * (sums[1] / all_chan)) * inv_std
    ).astype(jnp.bfloat16)
    near, far = pair_grad[:, :, :block_len], pair_grad[:, :, block_len:]
    none = jnp.zeros((), pair_grad.dtype)
    pair_grad = jnp.concatenate(
        [
            jnp.where(
                at_own[:, b][None, :, None],
                near,
                jnp.where(at_other[:, b][None, :, None], far, none),
            )
            for b in range(blocks)
        ],
        axis=2,
    )

    weight_total = jnp.einsum("ckn,hkn->ch", normed, grads, preferred_element_type=jnp.float32)
    moment = jnp.einsum("ckn,hkn->ch", standard_near, grads, preferred_element_type=jnp.float32)
    wide = w_stacked.astype(jnp.float32)
    gain_terms = jnp.sum(wide * moment, axis=1)
    bias_terms = jnp.sum(wide * jnp.sum(grads.astype(jnp.float32), axis=(1, 2))[None, :], axis=1)
    vectors = by_channel(jnp.stack([gain_terms, bias_terms], axis=1))
    for bit in bits_down(chans):
        vectors = vectors + flip(vectors, "chan", bit)
    vectors = lax.dynamic_slice_in_dim(vectors, mine * part_chan, part_chan, 0)
    for bit in bits_down(ring):
        vectors = vectors + flip(vectors, "rows", bit)
        weight_total = weight_total + flip(weight_total, "rows", bit)
    factor = 1.0 / width
    weight_total = by_channel(weight_total) * factor
    vectors = vectors * factor
    return (pair_grad, vectors[:, 0], vectors[:, 1]) + tuple(jnp.split(weight_total, 4, axis=1))


def solution(mesh):
    in_specs = (
        P("chan", "rows", None),
        P("chan", "rows", None),
        P(),
        P(),
        P(),
        P(None, "chan"),
        P(None, "chan"),
        P(None, "chan"),
        P(None, "chan"),
    )
    out_specs = (
        P("chan", "rows", None),
        P("chan"),
        P("chan"),
        P(None, "chan"),
        P(None, "chan"),
        P(None, "chan"),
        P(None, "chan"),
    )
    return jax.shard_map(local, mesh=mesh, in_specs=in_specs, out_specs=out_specs, check_vma=False)
```

```python
import math

import jax
import jax.numpy as jnp
from jax import lax
from jax.sharding import PartitionSpec as P

EPS = 1e-05


def ring_order(count):
    return list(range(0, count, 2)) + list(range(1, count, 2))[::-1]


def flip(x, axis, bit):
    count = lax.axis_size(axis)
    return lax.ppermute(x, axis, [(d, d ^ bit) for d in range(count)])


def bits_down(count):
    bits = [1 << b for b in range(count.bit_length() - 1)]
    return bits[::-1]


def local(
    pair_act, pair_cot, contact, ln_gain, ln_bias, left_gate, left_value, right_gate, right_value
):
    part_chan, rows_here, width = pair_act.shape
    part_hid = pair_cot.shape[0]
    blocks = contact.shape[0]
    block_len = width // blocks
    chans = lax.axis_size("chan")
    ring = lax.axis_size("rows")
    all_chan = part_chan * chans
    mine = lax.axis_index("chan")
    row_first = lax.axis_index("rows") * rows_here
    piece = math.gcd(rows_here, block_len)
    pieces = rows_here // piece

    numbers = jnp.arange(blocks, dtype=jnp.int32)
    other = jnp.sum(contact * numbers[None, :], axis=1) - numbers
    paired = jnp.sum(contact, axis=1) > 1
    row_block = (row_first + jnp.arange(rows_here, dtype=jnp.int32)) // block_len
    at_own = row_block[:, None] == numbers[None, :]
    row_other = jnp.sum(jnp.where(at_own, other[None, :], 0), axis=1)
    row_paired = jnp.sum(jnp.where(at_own, paired[None, :].astype(jnp.int32), 0), axis=1) > 0
    at_other = (row_other[:, None] == numbers[None, :]) & row_paired[:, None]
    weight = jnp.concatenate(
        [
            jnp.ones((rows_here, block_len), jnp.float32),
            jnp.broadcast_to(
                row_paired.astype(jnp.float32)[:, None], (rows_here, block_len)
            ),
        ],
        axis=1,
    )

    def compact(x):
        def pick(at):
            out = jnp.zeros((x.shape[0], rows_here, block_len), x.dtype)
            for b in range(blocks):
                here = x[:, :, b * block_len : (b + 1) * block_len]
                out = jnp.where(at[:, b][None, :, None], here, out)
            return out

        return jnp.concatenate([pick(at_own), pick(at_other)], axis=2)

    cot = compact(pair_cot)
    own_cot, other_cot = cot[:, :, :block_len], cot[:, :, block_len:]
    order = ring_order(ring)
    place = [order.index(d) for d in range(ring)]
    order_table = jnp.array(order, jnp.int32)
    my_place = jnp.array(place, jnp.int32)[lax.axis_index("rows")]
    right_perm = [(order[i], order[(i + 1) % ring]) for i in range(ring)]
    left_perm = [(order[(i + 1) % ring], order[i]) for i in range(ring)]
    act = compact(pair_act)

    def go_round(x):
        half = x.shape[0] // 2
        top = ring // 2
        arrived = []
        going_right, going_left = x, x
        for step in range(1, top + 1):
            last = step == top and ring % 2 == 0
            if last:
                going_right, going_left = going_right[:half], going_left[half:]
            going_right = lax.ppermute(going_right, "rows", right_perm)
            going_left = lax.ppermute(going_left, "rows", left_perm)
            from_left = order_table[(my_place - step + ring) % ring] * rows_here
            from_right = order_table[(my_place + step) % ring] * rows_here
            arrived.append((going_right, 0, from_left))
            arrived.append((going_left, half if last else 0, from_right))
        here, _ = lax.optimization_barrier((x, arrived[0][0]))
        out = jnp.zeros((x.shape[0], width, x.shape[2]), x.dtype)
        out = lax.dynamic_update_slice(out, here, (0, row_first, 0))
        for block, first, at in arrived:
            out = lax.dynamic_update_slice(out, block, (first, at, 0))
        return out

    gathered = go_round(own_cot)
    reach = -(-(block_len - piece) // rows_here)
    window = [other_cot]
    for hop in range(1, min(reach, ring - 1) + 1):
        up = [(d, d + hop) for d in range(ring - hop)]
        down = [(d + hop, d) for d in range(ring - hop)]
        window = (
            [lax.ppermute(other_cot, "rows", up)]
            + window
            + [lax.ppermute(other_cot, "rows", down)]
        )
    window_first = row_first - (len(window) // 2) * rows_here
    window = jnp.concatenate(window, axis=1)
    owns = [(row_first + p * piece) // block_len for p in range(pieces)]
    seconds = [other[own] for own in owns]
    mutual_row = paired & paired[other] & (other[other] == numbers)

    def crossed(x):
        everywhere = go_round(x)
        return [
            jnp.where(
                mutual_row[own],
                lax.dynamic_slice(
                    everywhere, (0, second * block_len, 0), (part_hid, block_len, block_len)
                ),
                jnp.zeros((), x.dtype),
            )
            for own, second in zip(owns, seconds)
        ]

    def uncrossed(x):
        return [jnp.zeros((part_hid, block_len, block_len), x.dtype) for _ in owns]

    cross = lax.cond(jnp.any(mutual_row), crossed, uncrossed, other_cot)

    parts, offsets = [act], [0]
    for bit in bits_down(chans):
        parts = parts + [flip(x, "chan", bit) for x in parts]
        offsets = offsets + [o + bit for o in offsets]
    full_act = jnp.concatenate(parts, axis=0).astype(jnp.float32)
    partner = jnp.array(offsets, jnp.int32) ^ mine

    def by_partner(x):
        return x.reshape((chans, part_chan) + x.shape[1:])[partner].reshape(x.shape)

    slot_of = [offsets.index(o) for o in range(chans)]
    back_order = jnp.array(slot_of, jnp.int32)[jnp.arange(chans, dtype=jnp.int32) ^ mine]

    def by_channel(x):
        return x.reshape((chans, part_chan) + x.shape[1:])[back_order].reshape(x.shape)

    gain = by_partner(ln_gain)
    bias = by_partner(ln_bias)
    w_stacked = by_partner(
        jnp.concatenate([left_gate, left_value, right_gate, right_value], axis=1)
    )

    mean = jnp.mean(full_act, axis=0)
    inv_std = lax.rsqrt(jnp.mean(full_act * full_act, axis=0) - mean * mean + EPS)
    standard = (full_act - mean) * inv_std
    normed = (standard * gain[:, None, None] + bias[:, None, None]).astype(jnp.bfloat16)
    standard_near = standard.astype(jnp.bfloat16)
    projected = jnp.einsum("ch,ckn->hkn", w_stacked, normed, preferred_element_type=jnp.float32)
    left_logit, left_linear, right_logit, right_linear = jnp.split(projected, 4, axis=0)
    left_sigmoid = jax.nn.sigmoid(left_logit)
    right_sigmoid = jax.nn.sigmoid(right_logit)
    left = (weight * left_sigmoid * left_linear).astype(jnp.bfloat16)
    right = (weight * right_sigmoid * right_linear).astype(jnp.bfloat16)

    corners = []
    for own, second, back_cross in zip(owns, seconds, cross):
        size = (part_hid, block_len, block_len)
        top = jnp.concatenate(
            [
                lax.dynamic_slice(gathered, (0, own * block_len, 0), size),
                lax.dynamic_slice(window, (0, own * block_len - window_first, 0), size),
            ],
            axis=2,
        )
        low = jnp.concatenate(
            [back_cross, lax.dynamic_slice(gathered, (0, second * block_len, 0), size)], axis=2
        )
        corners.append(jnp.concatenate([top, low], axis=1))
    corner = jnp.stack(corners, axis=1)

    def cut(x):
        return x.reshape(part_hid, pieces, piece, 2 * block_len)

    grad_left = jnp.einsum(
        "hpkj,hpij->hpki", cut(right), corner, preferred_element_type=jnp.float32
    ).reshape(left.shape)
    grad_right = jnp.einsum(
        "hpki,hpij->hpkj", cut(left), corner, preferred_element_type=jnp.float32
    ).reshape(left.shape)
    keep_left = grad_left * weight
    keep_right = grad_right * weight
    grads = jnp.concatenate(
        [
            (keep_left * left_linear * left_sigmoid * (1.0 - left_sigmoid)).astype(jnp.bfloat16),
            (keep_left * left_sigmoid).astype(jnp.bfloat16),
            (keep_right * right_linear * right_sigmoid * (1.0 - right_sigmoid)).astype(
                jnp.bfloat16
            ),
            (keep_right * right_sigmoid).astype(jnp.bfloat16),
        ],
        axis=0,
    )

    def back(rows):
        return jnp.einsum("ch,hkn->ckn", rows, grads, preferred_element_type=jnp.float32)

    w_parts = {o: w_stacked[i * part_chan : (i + 1) * part_chan] for i, o in enumerate(offsets)}
    partial = {o: back(w_parts[o]) for o in offsets}
    first_sum = jnp.zeros(mean.shape, jnp.float32)
    second_sum = jnp.zeros(mean.shape, jnp.float32)
    for i, o in enumerate(offsets):
        span = slice(i * part_chan, (i + 1) * part_chan)
        scaled = partial[o] * gain[span][:, None, None]
        first_sum = first_sum + jnp.sum(scaled, axis=0)
        second_sum = second_sum + jnp.sum(scaled * standard[span], axis=0)
    sums = jnp.stack([first_sum, second_sum])
    late_grads = grads
    for bit in bits_down(chans)[::-1]:
        leaving = {o: partial[o].astype(jnp.bfloat16) for o in partial if o & bit}
        received = {o - bit: flip(x, "chan", bit) for o, x in leaving.items()}
        late_grads, _ = lax.optimization_barrier((late_grads, tuple(leaving.values())))
        partial = {o: partial[o] + x.astype(jnp.float32) for o, x in received.items()}
        sums = sums + flip(sums, "chan", bit)
    normed_grad = partial[0]
    scaled = normed_grad * gain[:part_chan][:, None, None]
    pair_grad = (
        (scaled - sums[0] / all_chan - standard[:part_chan] * (sums[1] / all_chan)) * inv_std
    ).astype(jnp.bfloat16)
    near, far = pair_grad[:, :, :block_len], pair_grad[:, :, block_len:]
    none = jnp.zeros((), pair_grad.dtype)
    pair_grad = jnp.concatenate(
        [
            jnp.where(
                at_own[:, b][None, :, None],
                near,
                jnp.where(at_other[:, b][None, :, None], far, none),
            )
            for b in range(blocks)
        ],
        axis=2,
    )

    weight_total = jnp.einsum("ckn,hkn->ch", normed, late_grads, preferred_element_type=jnp.float32)
    moment = jnp.einsum("ckn,hkn->ch", standard_near, late_grads, preferred_element_type=jnp.float32)
    wide = w_stacked.astype(jnp.float32)
    gain_terms = jnp.sum(wide * moment, axis=1)
    bias_terms = jnp.sum(wide * jnp.sum(late_grads.astype(jnp.float32), axis=(1, 2))[None, :], axis=1)
    vectors = by_channel(jnp.stack([gain_terms, bias_terms], axis=1))
    for bit in bits_down(chans):
        vectors = vectors + flip(vectors, "chan", bit)
    vectors = lax.dynamic_slice_in_dim(vectors, mine * part_chan, part_chan, 0)
    for bit in bits_down(ring):
        vectors = vectors + flip(vectors, "rows", bit)
        weight_total = weight_total + flip(weight_total, "rows", bit)
    factor = 1.0 / width
    weight_total = by_channel(weight_total) * factor
    vectors = vectors * factor
    return (pair_grad, vectors[:, 0], vectors[:, 1]) + tuple(jnp.split(weight_total, 4, axis=1))


def solution(mesh):
    in_specs = (
        P("chan", "rows", None),
        P("chan", "rows", None),
        P(),
        P(),
        P(),
        P(None, "chan"),
        P(None, "chan"),
        P(None, "chan"),
        P(None, "chan"),
    )
    out_specs = (
        P("chan", "rows", None),
        P("chan"),
        P("chan"),
        P(None, "chan"),
        P(None, "chan"),
        P(None, "chan"),
        P(None, "chan"),
    )
    return jax.shard_map(local, mesh=mesh, in_specs=in_specs, out_specs=out_specs, check_vma=False)
```
